32 devices in a mesh: row: 8 (over z, y), col: 4 (over x, core).
Axes of the slice: x: 2, y: 2, z: 4, core: 2. Of those that a mesh axis runs over, the one named last changes fastest.
Arguments:
- nodes: bfloat16 [10240, 512], P(('row', 'col')), may hold values from -6 to 6
- edges: bfloat16 [65536, 512], P(('row', 'col')), may hold values from -6 to 6
- sender_slot: int32 [65536], P(('row', 'col')), may hold values from 0 to 575, as said below
- receiver: int32 [65536], P(('row', 'col')), may hold values from 0 to 319
- send_list: int32 [32, 256], P(('row', 'col')), may hold values from 0 to 319
- w_edge_in: bfloat16 [1536, 512], replicated, may hold values from -0.15625 to 0.15625
- b_edge: float32 [512], replicated, may hold values from -4 to 4
- w_edge_out: bfloat16 [512, 512], replicated, may hold values from -1 to 1
- g_edge: float32 [512], replicated, may hold values from 0.1 to 1.9
- w_node_in: bfloat16 [1024, 512], replicated, may hold values from -0.1875 to 0.1875
- b_node: float32 [512], replicated, may hold values from -4 to 4
- w_node_out: bfloat16 [512, 512], replicated, may hold values from -1 to 1
- g_node: float32 [512], replicated, may hold values from 0.1 to 1.9
- grad_nodes_out: bfloat16 [10240, 512], P(('row', 'col')), may hold values from -6 to 6
- grad_edges_out: bfloat16 [65536, 512], P(('row', 'col')), may hold values from -6 to 6
Outputs:
- new_nodes: bfloat16 [10240, 512], P(('row', 'col'))
- new_edges: bfloat16 [65536, 512], P(('row', 'col'))
- grad_nodes: float32 [10240, 512], P(('row', 'col'))
- grad_edges: bfloat16 [65536, 512], P(('row', 'col'))
The draws below stay inside these ranges and needn't reach their ends.
Inputs may be any that keep to these rules, and one draw needn't show every extreme that they name: `sender_slot`: A value 320 + p * 8 + c on an edge of device d never has p = d.
All inputs are finite; a program needn't handle non-finite values.
Results may differ from the reference program's by a relative error of at most 0.0085.
Values may be sent and summed in bfloat16 or wider, within the bound.
A program may use at most 128 MiB of HBM per device.

```python
import math
import jax
import jax.numpy as jnp
from jax import lax

D = 512
NODE_DEV = 320
EDGE_DEV = 2048
CAP = 8
NODES = 10240
EDGES = 65536
N_ROW = 8
N_COL = 4


def halo_graph(key):
    devices_all = N_ROW * N_COL
    key_count, key_busy, key_list, key_local, key_order = jax.random.split(jax.random.fold_in(key, 5), 5)
    counts = jax.random.randint(key_count, (devices_all, devices_all), 0, CAP + 1)
    busiest = jax.random.randint(key_busy, (), 0, devices_all)
    source_dev = jnp.arange(devices_all)[:, None]
    dest_dev = jnp.arange(devices_all)[None, :]
    counts = jnp.where(dest_dev == busiest, CAP, counts)
    counts = jnp.where(source_dev == dest_dev, 0, counts)
    send_list = jax.random.randint(key_list, (devices_all, devices_all * CAP), 0, NODE_DEV)
    position = jnp.arange(CAP)
    live_slots = (position[None, None, :] < counts.T[:, :, None]).reshape(devices_all, devices_all * CAP)
    live_slots = jnp.concatenate([live_slots, jnp.zeros((devices_all, EDGE_DEV - devices_all * CAP), dtype=bool)], axis=1)
    local_rows = jax.random.randint(key_local, (devices_all, EDGE_DEV), 0, NODE_DEV)
    slot_ids = NODE_DEV + jnp.arange(EDGE_DEV)
    slot_plan = jnp.where(live_slots, slot_ids[None, :], local_rows)

    def shuffle(one_key):
        return jax.random.permutation(one_key, EDGE_DEV)
    orders = jax.vmap(shuffle)(jax.random.split(key_order, devices_all))
    sender_slot = jnp.take_along_axis(slot_plan, orders, axis=1).reshape(devices_all * EDGE_DEV)
    return (send_list.astype(jnp.int32), sender_slot.astype(jnp.int32))


def draw_send_list(key, part):
    return halo_graph(key)[0]


def draw_sender_slot(key, part):
    return halo_graph(key)[1]


def column_scaled(key):
    key_base, key_scale = jax.random.split(key)
    base_vals = jnp.clip(jax.random.normal(key_base, (D, D), jnp.float32), -6.0, 6.0)
    scales = jnp.exp(jax.random.uniform(key_scale, (1, D), jnp.float32, math.log(0.3), math.log(3.0)))
    return jnp.clip(base_vals * scales / math.sqrt(D), -1.0, 1.0).astype(jnp.bfloat16)


def draw_w_edge_out(key, part):
    return column_scaled(jax.random.fold_in(key, 11))


def draw_w_node_out(key, part):
    return column_scaled(jax.random.fold_in(key, 13))


def plant(result, stream_key, low, largest):
    shape = result.shape
    index_at = [jax.random.randint(jax.random.fold_in(stream_key, axis), (), 0, shape[axis]) for axis in range(len(shape))]
    result = result.at[tuple(index_at)].set(low)
    longest = shape.index(max(shape))
    index_at[longest] = (index_at[longest] + 1) % shape[longest]
    return result.at[tuple(index_at)].set(largest)


def level_of(rng, shape, cuts, least, top_value):
    gain, own = 1.0, jax.random.fold_in(rng, 6)
    for dim, shards_of in cuts:
        steps = jnp.exp(jax.random.uniform(jax.random.fold_in(own, dim), (shards_of,), jnp.float32, least / len(cuts), top_value / len(cuts)))
        gain = gain * jnp.repeat(steps, shape[dim] // shards_of).reshape([-1 if axis == dim else 1 for axis in range(len(shape))])
    return gain


def normal_values(key, shape, width, limit, cuts=(), kind=jnp.bfloat16):
    values = jax.random.normal(key, shape, jnp.float32) * width
    if len(cuts) > 0:
        values = level_of(key, shape, cuts, -0.22, 0.18) * values
    return jnp.clip(values, min=-limit, max=limit).astype(kind)


def setup_inputs(seed: int = 0) -> dict:
    key_of = jax.random.split(jax.random.key(seed), 16)
    return {
        "nodes": normal_values(key_of[0], (NODES, D), 1.0, 6.0, ((0, 32),)),
        "edges": normal_values(key_of[1], (EDGES, D), 1.0, 6.0, ((0, 32),)),
        "sender_slot": draw_sender_slot(jax.random.fold_in(key_of[15], 71), 0),
        "receiver": plant(jax.random.randint(key_of[3], (EDGES,), 0, NODE_DEV), jax.random.fold_in(key_of[3], 1), 0, NODE_DEV - 1).astype(jnp.int32),
        "send_list": draw_send_list(jax.random.fold_in(key_of[15], 71), 0),
        "w_edge_in": normal_values(key_of[5], (3 * D, D), (3 * D) ** -0.5, 0.15625),
        "b_edge": normal_values(key_of[6], (D,), 1.0, 4.0, (), jnp.float32),
        "w_edge_out": draw_w_edge_out(jax.random.fold_in(key_of[15], 71), 0),
        "g_edge": jnp.clip(1.0 + 0.18 * jax.random.normal(key_of[8], (D,), jnp.float32), 0.1, 1.9),
        "w_node_in": normal_values(key_of[9], (2 * D, D), (2 * D) ** -0.5, 0.1875),
        "b_node": normal_values(key_of[10], (D,), 1.0, 4.0, (), jnp.float32),
        "w_node_out": draw_w_node_out(jax.random.fold_in(key_of[15], 71), 0),
        "g_node": jnp.clip(1.0 + 0.18 * jax.random.normal(key_of[12], (D,), jnp.float32), 0.1, 1.9),
        "grad_nodes_out": normal_values(key_of[13], (NODES, D), 1.0, 6.0, ((0, 32),)),
        "grad_edges_out": normal_values(key_of[14], (EDGES, D), 1.0, 6.0, ((0, 32),)),
    }


norm_eps = 1e-05

def perceptron(pieces, weight_in, bias_vec, weight_out, gain_vec):
    joined = jnp.concatenate(pieces, axis=1)
    pre_act = jnp.dot(joined, weight_in, preferred_element_type=jnp.float32) + bias_vec
    activated = jax.nn.silu(pre_act).astype(jnp.bfloat16)
    hidden = jnp.dot(activated, weight_out, preferred_element_type=jnp.float32)
    row_mean = lax.optimization_barrier(jnp.mean(hidden, axis=-1, keepdims=True))
    centred = hidden - row_mean
    variance = lax.optimization_barrier(jnp.mean(centred * centred, axis=-1, keepdims=True))
    inv_std = lax.rsqrt(variance + norm_eps)
    normed = centred * inv_std
    return (pre_act, normed, inv_std, normed * gain_vec)

def perceptron_grad(upstream, pre_act, normed, inv_std, weight_out, gain_vec):
    scaled = upstream * gain_vec
    d_hidden = inv_std * (scaled - lax.optimization_barrier(jnp.mean(scaled, axis=-1, keepdims=True)) - normed * lax.optimization_barrier(jnp.mean(scaled * normed, axis=-1, keepdims=True)))
    d_hidden = d_hidden.astype(jnp.bfloat16)
    d_act = jnp.dot(d_hidden, weight_out.T, preferred_element_type=jnp.float32)
    sigmoid_v = jax.nn.sigmoid(pre_act)
    return (d_act * sigmoid_v * (1.0 + pre_act * (1.0 - sigmoid_v))).astype(jnp.bfloat16)

def reference(nodes, edges, sender_slot, receiver, send_list, w_edge_in, b_edge, w_edge_out, g_edge, w_node_in, b_node, w_node_out, g_node, grad_nodes_out, grad_edges_out):
    device_count = N_ROW * N_COL
    total_nodes, feature_width = nodes.shape
    edge_total = edges.shape[0]
    owner = (jnp.arange(edge_total, dtype=jnp.int32) // EDGE_DEV).astype(jnp.int32)
    remote = jnp.maximum(sender_slot - NODE_DEV, 0).astype(jnp.int32)
    source_dev = (remote // CAP).astype(jnp.int32)
    source_col = (remote % CAP).astype(jnp.int32)
    listed = send_list[source_dev, owner * CAP + source_col]
    sender = jnp.where(sender_slot < NODE_DEV, owner * NODE_DEV + sender_slot, source_dev * NODE_DEV + listed).astype(jnp.int32)
    target = (owner * NODE_DEV + receiver).astype(jnp.int32)
    senders = nodes[sender]
    targets = nodes[target]

    def blocks(array):
        return array.reshape((device_count, EDGE_DEV) + array.shape[1:])

    def forward_block(pieces):
        return perceptron(list(pieces), w_edge_in, b_edge, w_edge_out, g_edge)[3]
    message = lax.map(forward_block, (blocks(edges), blocks(senders), blocks(targets)))
    message = message.reshape(edge_total, feature_width)
    new_edges = (edges.astype(jnp.float32) + message).astype(jnp.bfloat16)
    incoming = jax.ops.segment_sum(message, target, num_segments=total_nodes).astype(jnp.bfloat16)
    pre_node, normed_node, inv_node, update = perceptron([nodes, incoming], w_node_in, b_node, w_node_out, g_node)
    new_nodes = (nodes.astype(jnp.float32) + update).astype(jnp.bfloat16)
    d_pre_node = perceptron_grad(grad_nodes_out.astype(jnp.float32), pre_node, normed_node, inv_node, w_node_out, g_node)
    d_node_in = jnp.dot(d_pre_node, w_node_in.T, preferred_element_type=jnp.float32)
    d_own = d_node_in[:, :feature_width]
    d_incoming = d_node_in[:, feature_width:]
    d_message = grad_edges_out.astype(jnp.float32) + d_incoming[target]

    def backward_block(pieces):
        edge_part, sender_part, target_part, upstream, given = pieces
        pre_act, normed, inv_std, unused = perceptron([edge_part, sender_part, target_part], w_edge_in, b_edge, w_edge_out, g_edge)
        d_pre = perceptron_grad(upstream, pre_act, normed, inv_std, w_edge_out, g_edge)
        d_in = jnp.dot(d_pre, w_edge_in.T, preferred_element_type=jnp.float32)
        grad_part = (given.astype(jnp.float32) + d_in[:, :feature_width]).astype(jnp.bfloat16)
        return (grad_part, d_in[:, feature_width:2 * feature_width], d_in[:, 2 * feature_width:])
    grad_edges, d_from, d_to = lax.map(backward_block, (blocks(edges), blocks(senders), blocks(targets), blocks(d_message), blocks(grad_edges_out)))
    grad_edges = grad_edges.reshape(edge_total, feature_width)
    d_from = d_from.reshape(edge_total, feature_width)
    d_to = d_to.reshape(edge_total, feature_width)
    grad_nodes = grad_nodes_out.astype(jnp.float32) + d_own + jax.ops.segment_sum(d_to, target, num_segments=total_nodes) + jax.ops.segment_sum(d_from, sender, num_segments=total_nodes)
    return (new_nodes, new_edges, grad_nodes, grad_edges)
```

```python
import functools

import jax
import jax.numpy as jnp
from jax import lax
from jax.experimental import pallas as pl
from jax.experimental.pallas import tpu as pltpu
from jax.sharding import PartitionSpec as P

norm_eps = 1e-05
LANES = 128
TILE = 256
MESH = pl.DeviceIdType.MESH
f32 = jnp.float32
bf16 = jnp.bfloat16


def mm(left, right):
    return jnp.dot(left, right, preferred_element_type=f32)


def mm_t(left, right):
    return lax.dot_general(left, right, (((1,), (1,)), ((), ())), preferred_element_type=f32)


def sigmoid(value):
    return 0.5 * jnp.tanh(0.5 * value) + 0.5


def row_mean(value):
    return jnp.mean(value, axis=-1, keepdims=True)


def normalize(value):
    centred = value - row_mean(value)
    inv_std = lax.rsqrt(row_mean(centred * centred) + norm_eps)
    return centred * inv_std, inv_std


def norm_grad(upstream, gain, normed, inv_std):
    scaled = upstream * gain
    return (inv_std * (scaled - row_mean(scaled) - normed * row_mean(scaled * normed))).astype(bf16)


def ones_where(mask):
    return jnp.where(mask, 1.0, 0.0).astype(bf16)


def as_column(row):
    return jnp.transpose(jnp.broadcast_to(row, (LANES, row.shape[1])))


def kernel(
    sizes,
    nodes, slot, recv, listing, b_e, g_e, b_n, g_n, gno,
    edges, geo, w_ei_h, w_eo_h, w_ni_h, w_no_h,
    new_nodes, grad_nodes, new_edges, grad_edges,
    ebuf, gbuf, w_ei, w_eo, w_ni, w_no, npad, table, picks, picks_t,
    pre_s, nrm_s, inv_s, nebuf, dpbuf, inc, dinc, racc, lacc,
    outgoing, arrived, sums, returned,
    sem_w, sem_e, sem_g, sem_ne, sem_ge, send1, recv1, send2, recv2,
):
    rows, cols, cap = sizes
    peers = rows * cols
    n, d = nodes.shape
    tiles, _, tile = slot.shape
    remote = peers * cap
    width = remote + 2 * n
    n_pad = npad.shape[0]
    my_row, my_col = lax.axis_index("row"), lax.axis_index("col")
    me = my_row * cols + my_col

    def span(t):
        return pl.ds(pl.multiple_of(t * tile, tile), tile)

    def coords(k):
        peer = lax.rem(me + k, peers)
        return peer, (peer // cols, lax.rem(peer, cols))

    barrier = pltpu.get_barrier_semaphore()

    def greet(k, carry):
        pl.semaphore_signal(barrier, inc=1, device_id=coords(k)[1], device_id_type=MESH)
        return carry

    lax.fori_loop(1, peers, greet, 0)

    def load_edges(t):
        return pltpu.make_async_copy(edges.at[span(t)], ebuf.at[span(t)], sem_e.at[t])

    def load_grads(t):
        return pltpu.make_async_copy(geo.at[span(t)], gbuf.at[span(t)], sem_g.at[t])

    def store_edges(t):
        return pltpu.make_async_copy(nebuf.at[span(t)], new_edges.at[span(t)], sem_ne.at[t])

    def store_grads(t):
        return pltpu.make_async_copy(gbuf.at[span(t)], grad_edges.at[span(t)], sem_ge.at[t])

    load_w = [
        pltpu.make_async_copy(src, dst, sem_w.at[i])
        for i, (src, dst) in enumerate(((w_ei_h, w_ei), (w_eo_h, w_eo), (w_ni_h, w_ni), (w_no_h, w_no)))
    ]
    load_w[0].start()
    for t in range(tiles):
        load_edges(t).start()
    for copy in load_w[1:]:
        copy.start()
    for t in range(tiles):
        load_grads(t).start()

    npad[:n] = nodes[...]
    if n_pad > n:
        npad[n:] = jnp.zeros((n_pad - n, d), bf16)
        dinc[n:] = jnp.zeros((n_pad - n, d), bf16)
    lists = listing[...]
    list_col = as_column(lists)
    lane = lax.broadcasted_iota(jnp.int32, (remote, LANES), 1)
    list_pick = jnp.concatenate(
        [ones_where(lane + k == list_col) for k in range(0, n_pad, LANES)], axis=1
    )
    outgoing[...] = mm(list_pick, npad[...]).reshape(peers, cap, d).astype(bf16)
    arrived[me] = jnp.zeros((cap, d), bf16)
    returned[me] = jnp.zeros((cap, d), bf16)
    inc[...] = jnp.zeros_like(inc)
    racc[...] = jnp.zeros_like(racc)
    lacc[...] = jnp.zeros_like(lacc)

    def exchange(src, dst, send, got):
        def push(k, carry):
            peer, where = coords(k)
            pltpu.make_async_remote_copy(
                src_ref=src.at[peer], dst_ref=dst.at[me], send_sem=send, recv_sem=got,
                device_id=where, device_id_type=MESH,
            ).start()
            return carry

        lax.fori_loop(1, peers, push, 0)

    def whole(src, dst, send, got):
        part = pl.ds(0, peers - 1)
        return pltpu.make_async_remote_copy(
            src_ref=src.at[part], dst_ref=dst.at[part], send_sem=send, recv_sem=got,
            device_id=coords(1)[1], device_id_type=MESH,
        )

    pl.semaphore_wait(barrier, peers - 1)
    exchange(outgoing, arrived, send1, recv1)

    load_w[0].wait()
    table[remote : remote + n] = mm(nodes[...], w_ei[2 * d :]).astype(bf16)
    table[remote + n :] = mm(nodes[...], w_ei[d : 2 * d]).astype(bf16)

    def first(t, carry):
        sender = slot[t]
        c1 = jnp.where(sender >= n, sender - n, sender + (remote + n))
        c2 = recv[t] + remote
        rows_at = lax.broadcasted_iota(jnp.int32, (width, tile), 0)
        picks_t[t] = ones_where((rows_at == c1) | (rows_at == c2))
        c1c, c2c = as_column(c1), as_column(c2)
        lanes_at = lax.broadcasted_iota(jnp.int32, (tile, LANES), 1)
        for k in range(0, width, LANES):
            if k < remote:
                mask = lanes_at + k == c1c
            else:
                mask = (lanes_at + k == c1c) | (lanes_at + k == c2c)
            picks[span(t), k : k + LANES] = ones_where(mask)
        load_edges(t).wait()
        pre_s[span(t)] = (
            mm(ebuf[span(t)], w_ei[:d]) + mm(picks[span(t), remote:], table[remote:]) + b_e[...]
        )
        return carry

    lax.fori_loop(0, tiles, first, 0)

    whole(outgoing, arrived, send1, recv1).wait_recv()
    landed = arrived[...].astype(f32).reshape(remote, d).astype(bf16)
    table[:remote] = mm(landed, w_ei[d : 2 * d]).astype(bf16)
    load_w[1].wait()

    def second(t, carry):
        pre = pre_s[span(t)] + mm(picks[span(t), :remote], table[:remote])
        q = sigmoid(pre)
        pre_s[span(t)] = q * (1.0 + pre * (1.0 - q))
        normed, inv_std = normalize(mm((pre * q).astype(bf16), w_eo[...]))
        nrm_s[span(t)] = normed
        inv_s[span(t)] = inv_std
        message = normed * g_e[...]
        nebuf[span(t)] = (ebuf[span(t)].astype(f32) + message).astype(bf16)
        store_edges(t).start()
        inc[...] += mm(picks_t[t, remote : remote + n], message.astype(bf16))
        return carry

    lax.fori_loop(0, tiles, second, 0)

    load_w[2].wait()
    load_w[3].wait()
    pre = mm(nodes[...], w_ni[:d]) + mm(inc[...].astype(bf16), w_ni[d:]) + b_n[...]
    q = sigmoid(pre)
    normed, inv_std = normalize(mm((pre * q).astype(bf16), w_no[...]))
    new_nodes[...] = (nodes[...].astype(f32) + normed * g_n[...]).astype(bf16)
    given = gno[...].astype(f32)
    d_mid = norm_grad(given, g_n[...], normed, inv_std)
    d_pre = (mm_t(d_mid, w_no[...]) * (q * (1.0 + pre * (1.0 - q)))).astype(bf16)
    dinc[:n] = mm_t(d_pre, w_ni[d:]).astype(bf16)
    grad_nodes[...] = given + mm_t(d_pre, w_ni[:d])

    def third(t, carry):
        load_grads(t).wait()
        upstream = gbuf[span(t)].astype(f32) + mm(picks[span(t), remote : remote + n_pad], dinc[...])
        d_hid = norm_grad(upstream, g_e[...], nrm_s[span(t)], inv_s[span(t)])
        d_in = (mm_t(d_hid, w_eo[...]) * pre_s[span(t)]).astype(bf16)
        dpbuf[span(t)] = d_in
        racc[...] += mm(picks_t[t, :remote], d_in)
        return carry

    lax.fori_loop(0, tiles, third, 0)
    sums[...] = racc[...].reshape(peers, cap, d).astype(bf16)
    exchange(sums, returned, send2, recv2)

    def fourth(t, carry):
        d_in = dpbuf[span(t)]
        gbuf[span(t)] = (gbuf[span(t)].astype(f32) + mm_t(d_in, w_ei[:d])).astype(bf16)
        store_grads(t).start()
        lacc[...] += mm(picks_t[t, remote:], d_in)
        return carry

    lax.fori_loop(0, tiles, fourth, 0)
    grad_nodes[...] += mm_t(lacc[:n].astype(bf16), w_ei[2 * d :])

    whole(sums, returned, send2, recv2).wait_recv()
    back = returned[...].astype(f32).reshape(remote, d).astype(bf16)
    list_pick_t = ones_where(lax.broadcasted_iota(jnp.int32, (n, remote), 0) == lists)
    owned = lacc[n:] + mm(list_pick_t, back)
    grad_nodes[...] += mm_t(owned.astype(bf16), w_ei[d : 2 * d])

    whole(outgoing, arrived, send1, recv1).wait_send()
    whole(sums, returned, send2, recv2).wait_send()
    for t in range(tiles):
        store_edges(t).wait()
        store_grads(t).wait()


def local(
    nodes, edges, sender_slot, receiver, send_list, w_edge_in, b_edge, w_edge_out, g_edge,
    w_node_in, b_node, w_node_out, g_node, grad_nodes_out, grad_edges_out,
):
    rows, cols = lax.axis_size("row"), lax.axis_size("col")
    peers = rows * cols
    n, d = nodes.shape
    e = edges.shape[0]
    cap = send_list.shape[1] // peers
    remote = peers * cap
    width = remote + 2 * n
    tile = TILE
    tiles = e // tile
    n_pad = -(-n // LANES) * LANES
    assert e % tile == 0 and remote % LANES == 0 and width % LANES == 0 and n_pad <= 2 * n
    vmem = pl.BlockSpec(memory_space=pltpu.VMEM)
    hbm = pl.BlockSpec(memory_space=pl.ANY)
    dma = pltpu.SemaphoreType.DMA
    new_nodes, grad_nodes, new_edges, grad_edges = pl.pallas_call(
        functools.partial(kernel, (rows, cols, cap)),
        out_shape=(
            jax.ShapeDtypeStruct((n, d), bf16),
            jax.ShapeDtypeStruct((n, d), f32),
            jax.ShapeDtypeStruct((e, d), bf16),
            jax.ShapeDtypeStruct((e, d), bf16),
        ),
        in_specs=[vmem] * 9 + [hbm] * 6,
        out_specs=(vmem, vmem, hbm, hbm),
        scratch_shapes=[
            pltpu.VMEM((e, d), bf16),
            pltpu.VMEM((e, d), bf16),
            pltpu.VMEM(w_edge_in.shape, bf16),
            pltpu.VMEM(w_edge_out.shape, bf16),
            pltpu.VMEM(w_node_in.shape, bf16),
            pltpu.VMEM(w_node_out.shape, bf16),
            pltpu.VMEM((n_pad, d), bf16),
            pltpu.VMEM((width, d), bf16),
            pltpu.VMEM((e, width), bf16),
            pltpu.VMEM((tiles, width, tile), bf16),
            pltpu.VMEM((e, d), f32),
            pltpu.VMEM((e, d), f32),
            pltpu.VMEM((e, 1), f32),
            pltpu.VMEM((e, d), bf16),
            pltpu.VMEM((e, d), bf16),
            pltpu.VMEM((n, d), f32),
            pltpu.VMEM((n_pad, d), bf16),
            pltpu.VMEM((remote, d), f32),
            pltpu.VMEM((2 * n, d), f32),
            pltpu.VMEM((peers, cap, d), bf16),
            pltpu.VMEM((peers, cap, d), bf16),
            pltpu.VMEM((peers, cap, d), bf16),
            pltpu.VMEM((peers, cap, d), bf16),
            dma((4,)),
            dma((tiles,)),
            dma((tiles,)),
            dma((tiles,)),
            dma((tiles,)),
            dma, dma, dma, dma,
        ],
        compiler_params=pltpu.CompilerParams(
            collective_id=0, has_side_effects=True, vmem_limit_bytes=60 * 1024 * 1024
        ),
        name="round",
    )(
        nodes,
        sender_slot.reshape(tiles, 1, tile),
        receiver.reshape(tiles, 1, tile),
        send_list,
        b_edge.reshape(1, d),
        g_edge.reshape(1, d),
        b_node.reshape(1, d),
        g_node.reshape(1, d),
        grad_nodes_out,
        edges, grad_edges_out, w_edge_in, w_edge_out, w_node_in, w_node_out,
    )
    return new_nodes, new_edges, grad_nodes, grad_edges


def solution(mesh):
    split = P(("row", "col"), None)
    flat = P(("row", "col"))
    whole = P()
    in_specs = (split, split, flat, flat, split) + (whole,) * 8 + (split, split)
    return jax.shard_map(
        local, mesh=mesh, in_specs=in_specs, out_specs=(split,) * 4, check_vma=False
    )
```

```python
import functools

import jax
import jax.numpy as jnp
from jax import lax
from jax.experimental import pallas as pl
from jax.experimental.pallas import tpu as pltpu
from jax.sharding import PartitionSpec as P

norm_eps = 1e-05
LANES = 128
TILE = 512
CHUNK = 512
MESH = pl.DeviceIdType.MESH
f32 = jnp.float32
bf16 = jnp.bfloat16


def mm(left, right):
    return jnp.dot(left, right, preferred_element_type=f32)


def mm_t(left, right):
    return lax.dot_general(left, right, (((1,), (1,)), ((), ())), preferred_element_type=f32)


def sigmoid(value):
    return 0.5 * jnp.tanh(0.5 * value) + 0.5


def row_mean(value):
    return jnp.mean(value, axis=-1, keepdims=True)


def normalize(value):
    centred = value - row_mean(value)
    inv_std = lax.rsqrt(row_mean(centred * centred) + norm_eps)
    return centred * inv_std, inv_std


def norm_grad(upstream, gain, normed, inv_std):
    scaled = upstream * gain
    return (inv_std * (scaled - row_mean(scaled) - normed * row_mean(scaled * normed))).astype(bf16)


def ones_where(mask):
    return jnp.where(mask, 1.0, 0.0).astype(bf16)


def as_column(row):
    return jnp.transpose(jnp.broadcast_to(row, (LANES, row.shape[1])))


def kernel(
    sizes,
    nodes, slot, recv, listing, b_e, g_e, b_n, g_n, gno,
    edges, geo, w_ei_h, w_eo_h, w_ni_h, w_no_h,
    new_nodes, grad_nodes, new_edges, grad_edges,
    ebuf, gbuf, w_ei, w_eo, w_ni, w_no, npad, table, picks, picks_t,
    pre_s, nrm_s, inv_s, nebuf, dpbuf, inc, dinc, racc, lacc,
    outgoing, arrived, sums, returned,
    sem_w, sem_e, sem_g, sem_ne, sem_ge, send1, recv1, send2, recv2,
):
    rows, cols, cap = sizes
    peers = rows * cols
    n, d = nodes.shape
    tiles, _, tile = slot.shape
    remote = peers * cap
    width = remote + 2 * n
    n_pad = npad.shape[0]
    my_row, my_col = lax.axis_index("row"), lax.axis_index("col")
    me = my_row * cols + my_col

    def span(t):
        return pl.ds(pl.multiple_of(t * tile, tile), tile)

    def coords(k):
        peer = lax.rem(me + k, peers)
        return peer, (peer // cols, lax.rem(peer, cols))

    barrier = pltpu.get_barrier_semaphore()

    def greet(k, carry):
        pl.semaphore_signal(barrier, inc=1, device_id=coords(k)[1], device_id_type=MESH)
        return carry

    lax.fori_loop(1, peers, greet, 0)

    def load_edges(t):
        return pltpu.make_async_copy(edges.at[span(t)], ebuf.at[span(t)], sem_e.at[t])

    def load_grads(t):
        return pltpu.make_async_copy(geo.at[span(t)], gbuf.at[span(t)], sem_g.at[t])

    def store_edges(t):
        return pltpu.make_async_copy(nebuf.at[span(t)], new_edges.at[span(t)], sem_ne.at[t])

    def store_grads(t):
        return pltpu.make_async_copy(gbuf.at[span(t)], grad_edges.at[span(t)], sem_ge.at[t])

    load_w = [
        pltpu.make_async_copy(src, dst, sem_w.at[i])
        for i, (src, dst) in enumerate(((w_ei_h, w_ei), (w_eo_h, w_eo), (w_ni_h, w_ni), (w_no_h, w_no)))
    ]
    load_w[0].start()
    for t in range(tiles):
        load_edges(t).start()
    for copy in load_w[1:]:
        copy.start()
    for t in range(tiles):
        load_grads(t).start()

    npad[:n] = nodes[...]
    if n_pad > n:
        npad[n:] = jnp.zeros((n_pad - n, d), bf16)
        dinc[n:] = jnp.zeros((n_pad - n, d), bf16)
    lists = listing[...]
    list_col = as_column(lists)
    lane = lax.broadcasted_iota(jnp.int32, (remote, LANES), 1)
    list_pick = jnp.concatenate(
        [ones_where(lane + k == list_col) for k in range(0, n_pad, LANES)], axis=1
    )
    outgoing[...] = mm(list_pick, npad[...]).reshape(peers, cap, d).astype(bf16)
    arrived[me] = jnp.zeros((cap, d), bf16)
    returned[me] = jnp.zeros((cap, d), bf16)
    inc[...] = jnp.zeros_like(inc)
    racc[...] = jnp.zeros_like(racc)
    lacc[...] = jnp.zeros_like(lacc)

    def exchange(src, dst, send, got):
        def push(k, carry):
            peer, where = coords(k)
            pltpu.make_async_remote_copy(
                src_ref=src.at[peer], dst_ref=dst.at[me], send_sem=send, recv_sem=got,
                device_id=where, device_id_type=MESH,
            ).start()
            return carry

        lax.fori_loop(1, peers, push, 0)

    def whole(src, dst, send, got):
        part = pl.ds(0, peers - 1)
        return pltpu.make_async_remote_copy(
            src_ref=src.at[part], dst_ref=dst.at[part], send_sem=send, recv_sem=got,
            device_id=coords(1)[1], device_id_type=MESH,
        )

    pl.semaphore_wait(barrier, peers - 1)
    exchange(outgoing, arrived, send1, recv1)

    load_w[0].wait()
    table[remote : remote + n] = mm(nodes[...], w_ei[2 * d :]).astype(bf16)
    table[remote + n :] = mm(nodes[...], w_ei[d : 2 * d]).astype(bf16)

    def first(t, carry):
        sender = slot[t]
        c1 = jnp.where(sender >= n, sender - n, sender + (remote + n))
        c2 = recv[t] + remote
        rows_at = lax.broadcasted_iota(jnp.int32, (width, tile), 0)
        picks_t[t] = ones_where((rows_at == c1) | (rows_at == c2))
        c1c, c2c = as_column(c1), as_column(c2)
        lanes_at = lax.broadcasted_iota(jnp.int32, (tile, LANES), 1)
        for k in range(0, width, LANES):
            if k < remote:
                mask = lanes_at + k == c1c
            else:
                mask = (lanes_at + k == c1c) | (lanes_at + k == c2c)
            picks[span(t), k : k + LANES] = ones_where(mask)
        load_edges(t).wait()
        pre_s[span(t)] = (
            mm(ebuf[span(t)], w_ei[:d]) + mm(picks[span(t), remote:], table[remote:]) + b_e[...]
        )
        return carry

    lax.fori_loop(0, tiles, first, 0)

    whole(outgoing, arrived, send1, recv1).wait_recv()
    landed = arrived[...].astype(f32).reshape(remote, d).astype(bf16)
    table[:remote] = mm(landed, w_ei[d : 2 * d]).astype(bf16)
    load_w[1].wait()

    def second(t, carry):
        pre = pre_s[span(t)] + mm(picks[span(t), :remote], table[:remote])
        q = sigmoid(pre)
        pre_s[span(t)] = q * (1.0 + pre * (1.0 - q))
        normed, inv_std = normalize(mm((pre * q).astype(bf16), w_eo[...]))
        nrm_s[span(t)] = normed
        inv_s[span(t)] = inv_std
        message = normed * g_e[...]
        nebuf[span(t)] = (ebuf[span(t)].astype(f32) + message).astype(bf16)
        store_edges(t).start()
        inc[...] += mm(picks_t[t, remote : remote + n], message.astype(bf16))
        return carry

    lax.fori_loop(0, tiles, second, 0)

    load_w[2].wait()
    load_w[3].wait()
    pre = mm(nodes[...], w_ni[:d]) + mm(inc[...].astype(bf16), w_ni[d:]) + b_n[...]
    q = sigmoid(pre)
    normed, inv_std = normalize(mm((pre * q).astype(bf16), w_no[...]))
    new_nodes[...] = (nodes[...].astype(f32) + normed * g_n[...]).astype(bf16)
    given = gno[...].astype(f32)
    d_mid = norm_grad(given, g_n[...], normed, inv_std)
    d_pre = (mm_t(d_mid, w_no[...]) * (q * (1.0 + pre * (1.0 - q)))).astype(bf16)
    dinc[:n] = mm_t(d_pre, w_ni[d:]).astype(bf16)
    grad_nodes[...] = given + mm_t(d_pre, w_ni[:d])

    def third(t, carry):
        load_grads(t).wait()
        upstream = gbuf[span(t)].astype(f32) + mm(picks[span(t), remote : remote + n_pad], dinc[...])
        d_hid = norm_grad(upstream, g_e[...], nrm_s[span(t)], inv_s[span(t)])
        d_in = (mm_t(d_hid, w_eo[...]) * pre_s[span(t)]).astype(bf16)
        dpbuf[span(t)] = d_in
        racc[...] += mm(picks_t[t, :remote], d_in)
        return carry

    lax.fori_loop(0, tiles, third, 0)
    sums[...] = racc[...].reshape(peers, cap, d).astype(bf16)
    exchange(sums, returned, send2, recv2)

    def fourth(t, carry):
        d_in = dpbuf[span(t)]
        gbuf[span(t)] = (gbuf[span(t)].astype(f32) + mm_t(d_in, w_ei[:d])).astype(bf16)
        store_grads(t).start()
        lacc[...] += mm(picks_t[t, remote:], d_in)
        return carry

    lax.fori_loop(0, tiles, fourth, 0)
    grad_nodes[...] += mm_t(lacc[:n].astype(bf16), w_ei[2 * d :])

    whole(sums, returned, send2, recv2).wait_recv()
    back = returned[...].astype(f32).reshape(remote, d).astype(bf16)
    list_pick_t = ones_where(lax.broadcasted_iota(jnp.int32, (n, remote), 0) == lists)
    owned = lacc[n:] + mm(list_pick_t, back)
    grad_nodes[...] += mm_t(owned.astype(bf16), w_ei[d : 2 * d])

    whole(outgoing, arrived, send1, recv1).wait_send()
    whole(sums, returned, send2, recv2).wait_send()
    for t in range(tiles):
        store_edges(t).wait()
        store_grads(t).wait()


def deliver(count, *refs):
    held, finals = refs[:count], refs[count : 2 * count]
    bufs, got, put = refs[2 * count : 3 * count], refs[3 * count], refs[3 * count + 1]
    loads, stores = [], []
    for source, final, buf in zip(held, finals, bufs):
        total = source.shape[0]
        step = CHUNK if total % CHUNK == 0 else total
        for at in range(0, total, step):
            part, i = pl.ds(at, step), len(loads)
            loads.append(pltpu.make_async_copy(source.at[part], buf.at[part], got.at[i]))
            stores.append(pltpu.make_async_copy(buf.at[part], final.at[part], put.at[i]))
    for load in loads:
        load.start()
    for load, store in zip(loads, stores):
        load.wait()
        store.start()
    for store in stores:
        store.wait()


def local(
    nodes, edges, sender_slot, receiver, send_list, w_edge_in, b_edge, w_edge_out, g_edge,
    w_node_in, b_node, w_node_out, g_node, grad_nodes_out, grad_edges_out,
):
    rows, cols = lax.axis_size("row"), lax.axis_size("col")
    peers = rows * cols
    n, d = nodes.shape
    e = edges.shape[0]
    cap = send_list.shape[1] // peers
    remote = peers * cap
    width = remote + 2 * n
    tile = TILE
    tiles = e // tile
    n_pad = -(-n // LANES) * LANES
    assert e % tile == 0 and remote % LANES == 0 and width % LANES == 0 and n_pad <= 2 * n
    vmem = pl.BlockSpec(memory_space=pltpu.VMEM)
    hbm = pl.BlockSpec(memory_space=pl.ANY)
    dma = pltpu.SemaphoreType.DMA
    new_nodes, grad_nodes, new_edges, grad_edges = pl.pallas_call(
        functools.partial(kernel, (rows, cols, cap)),
        out_shape=(
            jax.ShapeDtypeStruct((n, d), bf16),
            jax.ShapeDtypeStruct((n, d), f32),
            jax.ShapeDtypeStruct((e, d), bf16),
            jax.ShapeDtypeStruct((e, d), bf16),
        ),
        in_specs=[vmem] * 9 + [hbm] * 6,
        out_specs=(vmem, vmem, hbm, hbm),
        scratch_shapes=[
            pltpu.VMEM((e, d), bf16),
            pltpu.VMEM((e, d), bf16),
            pltpu.VMEM(w_edge_in.shape, bf16),
            pltpu.VMEM(w_edge_out.shape, bf16),
            pltpu.VMEM(w_node_in.shape, bf16),
            pltpu.VMEM(w_node_out.shape, bf16),
            pltpu.VMEM((n_pad, d), bf16),
            pltpu.VMEM((width, d), bf16),
            pltpu.VMEM((e, width), bf16),
            pltpu.VMEM((tiles, width, tile), bf16),
            pltpu.VMEM((e, d), f32),
            pltpu.VMEM((e, d), f32),
            pltpu.VMEM((e, 1), f32),
            pltpu.VMEM((e, d), bf16),
            pltpu.VMEM((e, d), bf16),
            pltpu.VMEM((n, d), f32),
            pltpu.VMEM((n_pad, d), bf16),
            pltpu.VMEM((remote, d), f32),
            pltpu.VMEM((2 * n, d), f32),
            pltpu.VMEM((peers, cap, d), bf16),
            pltpu.VMEM((peers, cap, d), bf16),
            pltpu.VMEM((peers, cap, d), bf16),
            pltpu.VMEM((peers, cap, d), bf16),
            dma((4,)),
            dma((tiles,)),
            dma((tiles,)),
            dma((tiles,)),
            dma((tiles,)),
            dma, dma, dma, dma,
        ],
        compiler_params=pltpu.CompilerParams(
            collective_id=0, has_side_effects=True, vmem_limit_bytes=60 * 1024 * 1024
        ),
        name="round",
    )(
        nodes,
        sender_slot.reshape(tiles, 1, tile),
        receiver.reshape(tiles, 1, tile),
        send_list,
        b_edge.reshape(1, d),
        g_edge.reshape(1, d),
        b_node.reshape(1, d),
        g_node.reshape(1, d),
        grad_nodes_out,
        edges, grad_edges_out, w_edge_in, w_edge_out, w_node_in, w_node_out,
    )
    results = (new_edges, grad_edges, new_nodes, grad_nodes)
    parts = sum(r.shape[0] // CHUNK if r.shape[0] % CHUNK == 0 else 1 for r in results)
    new_edges, grad_edges, new_nodes, grad_nodes = pl.pallas_call(
        functools.partial(deliver, len(results)),
        out_shape=tuple(jax.ShapeDtypeStruct(r.shape, r.dtype) for r in results),
        in_specs=[hbm] * len(results),
        out_specs=(hbm,) * len(results),
        scratch_shapes=[pltpu.VMEM(r.shape, r.dtype) for r in results] + [dma((parts,)), dma((parts,))],
        name="deliver",
    )(*results)
    return new_nodes, new_edges, grad_nodes, grad_edges


def solution(mesh):
    split = P(("row", "col"), None)
    flat = P(("row", "col"))
    whole = P()
    in_specs = (split, split, flat, flat, split) + (whole,) * 8 + (split, split)
    return jax.shard_map(
        local, mesh=mesh, in_specs=in_specs, out_specs=(split,) * 4, check_vma=False
    )
```
